32 devices in a mesh: expert: 8 (over y, x, core), dp: 4 (over z).
Axes of the slice: x: 2, y: 2, z: 4, core: 2. Of those that a mesh axis runs over, the one named last changes fastest.
Arguments:
- tokens: bfloat16 [4096, 2048], P(('expert', 'dp')), may hold values from -6 to 6
- out_grad: bfloat16 [4096, 2048], P(('expert', 'dp')), may hold values from -1.25 to 1.25
- expert_ids: int32 [4096, 8], P(('expert', 'dp')), may hold values from 0 to 15, all different within a row; in each aligned block of 128 rows (0 to 127, 128 to 255, ...) at most 72 rows name the same one
- route_weight: bfloat16 [4096, 8], P(('expert', 'dp')), may hold values from 0.099609375 to 1
- w_gate_up: bfloat16 [16, 2048, 768], P('expert'), may hold values from -0.125 to 0.125
- w_down: bfloat16 [16, 384, 2048], P('expert'), may hold values from -0.3125 to 0.3125
Outputs:
- d_tokens: bfloat16 [4096, 2048], P(('expert', 'dp'))
- d_route: bfloat16 [4096, 8], P(('expert', 'dp'))
- grad_gate_up: bfloat16 [16, 2048, 768], P('expert', 'dp')
- grad_down: bfloat16 [16, 384, 2048], P('expert', None, 'dp')
The draws below stay inside these ranges and needn't reach their ends.
Inputs may be any that keep to these rules, and one draw needn't show every extreme that they name: `expert_ids`: each row names 8 different experts. Among the 128 rows of one device (aligned blocks of 128 rows) no expert is named more than 72 times, and in every draw some expert is named exactly 72 times by the rows of some device.
All inputs are finite; a program needn't handle non-finite values.
Results may differ from the reference program's by a relative error of at most 0.012.
Values may be sent and summed in bfloat16 or wider, within the bound.
A program may use at most 128 MiB of HBM per device.

```python
import math
import jax
import jax.numpy as jnp
import numpy as np
from jax import lax

D = 2048
FF = 384
TOP = 8
TOK_DEV = 128
EXPERTS = 16
CAP = 72
TOKENS = 4096
N_EXPERT = 8
N_DP = 4


def block_scale(rng, dims, split, low, largest):
    def one(axis_at, parts):
        heights = jax.random.uniform(jax.random.fold_in(jax.random.fold_in(rng, 6), axis_at), (parts,), jnp.float32, low / len(split), largest / len(split))
        return jnp.repeat(jnp.exp(heights), dims[axis_at] // parts).reshape((-1,) + (1,) * (len(dims) - axis_at - 1))

    gain = one(*split[0])
    for cut in split[1:]:
        gain = gain * one(*cut)
    return gain


def shared_out(rng, own, number, rows, count, top, most, skew):
    ranking = jax.random.permutation(rng, count)
    heavy_load, usual = load_shares(count, rows * top, most, skew, True), load_shares(count, rows * top, most, skew, False)
    places = jnp.arange(count)

    def named(tallies, offset_by):
        used = int((tallies > 0).sum())
        fixed = max(1, used // 4)
        moved = fixed + (places - fixed + offset_by * (used - fixed)) % max(1, count - fixed)
        return jnp.zeros((count,), jnp.int32).at[ranking[jnp.where(places < fixed, places, moved)]].set(jnp.asarray(tallies, jnp.int32))

    tallies = jnp.where(number % 4 == 0, named(heavy_load, number // 4), named(usual, number - number // 4 - 1))
    mixed = jax.random.permutation(jax.random.fold_in(own, 3), count)
    source_of, receiver = mixed[0:count // 2 * 2:2], mixed[1:count // 2 * 2:2]
    margin = jnp.minimum(tallies[source_of] - 1, most - tallies[receiver]) // 2
    margin = jnp.where((source_of == ranking[0]) | (receiver == ranking[0]) | (tallies[receiver] == 0), 0, jnp.maximum(margin, 0))
    moved = jax.random.randint(jax.random.fold_in(own, 4), (count // 2,), 0, 1 << 20) % (margin + 1)
    tallies = tallies.at[source_of].add(-moved).at[receiver].add(moved)
    items = jnp.searchsorted(jnp.cumsum(tallies), jnp.arange(rows * top), side="right").astype(jnp.int32)
    listing = items.reshape(top, rows).T
    listing = listing[jax.random.permutation(jax.random.fold_in(own, 1), rows)]
    offset_by = jax.random.randint(jax.random.fold_in(own, 2), (rows, 1), 0, top)
    return jnp.take_along_axis(listing, (jnp.arange(top)[None, :] + offset_by) % top, axis=1)


def load_shares(number_of, total, most, slope, full):
    portions = [(1 << 20) // math.isqrt(standing ** slope) + 1 for standing in range(1, number_of + 1)]
    largest = most if full else min(most, max(-(-total // number_of), total * portions[0] // sum(portions)))
    least = 1 if total - largest >= number_of - 1 else 0
    holding, rest = [largest] + [least] * (number_of - 1), total - largest - least * (number_of - 1)
    while rest > 0:
        candidates = [i for i in range(1, number_of) if holding[i] < largest] or [i for i in range(1, number_of) if holding[i] < most]
        pool, remaining = sum([portions[i] for i in candidates]), rest
        for i in candidates:
            more = min(most - holding[i], max(1, remaining * portions[i] // pool), rest)
            holding[i] = holding[i] + more
            rest = rest - more
    return np.array(holding)


def bell_draw(stream_key, dims, spread, limit, pieces=(), kind=jnp.bfloat16):
    array = spread * jax.random.normal(stream_key, dims, jnp.float32)
    if pieces:
        array = array * block_scale(stream_key, dims, pieces, -0.22, 0.18)
    return jnp.clip(array, -limit, limit).astype(kind)


def setup_inputs(seed: int = 0) -> dict:
    arg_keys = jax.random.split(jax.random.key(seed), 7)
    tokens = bell_draw(arg_keys[0], (TOKENS, D), 1.0, 6.0, ((0, 32),))
    out_grad = bell_draw(arg_keys[1], (TOKENS, D), 0.2, 1.25, ((0, 32),))
    expert_ids_keys = jax.random.split(jax.random.fold_in(arg_keys[2], 1), TOKENS // TOK_DEV)
    expert_ids_turns = jax.random.permutation(jax.random.fold_in(arg_keys[2], 3), TOKENS // TOK_DEV)
    expert_ids = jax.vmap(lambda own, number: shared_out(jax.random.fold_in(arg_keys[2], 2), own, number, TOK_DEV, EXPERTS, TOP, CAP, 2))(expert_ids_keys, expert_ids_turns).reshape((TOKENS, TOP))
    route_weight = jnp.clip(0.099609375 + 0.9003906 * jax.random.uniform(arg_keys[3], (TOKENS, TOP), jnp.float32) ** block_scale(arg_keys[3], (TOKENS, TOP), ((0, 32),), -0.2, 0.2), 0.099609375, 1.0).astype(jnp.bfloat16)
    w_gate_up = bell_draw(arg_keys[4], (EXPERTS, D, 2 * FF), D ** -0.5, 0.125, ((0, 8),))
    w_down = bell_draw(arg_keys[5], (EXPERTS, FF, D), FF ** -0.5, 0.3125, ((0, 8),))
    return dict(tokens=tokens, out_grad=out_grad, expert_ids=expert_ids, route_weight=route_weight, w_gate_up=w_gate_up, w_down=w_down)


def expert_backward(rows_in, rows_grad, weight, gate_up, down):
    pre_act = jnp.dot(rows_in, gate_up, preferred_element_type=jnp.float32)
    half_width = pre_act.shape[1] // 2
    gate_pre = pre_act[:, :half_width]
    up_pre = pre_act[:, half_width:]
    sigmoid_gate = jax.nn.sigmoid(gate_pre)
    active = gate_pre * sigmoid_gate
    hidden = (active * up_pre).astype(jnp.bfloat16)
    back_hidden = lax.dot_general(rows_grad, down, (((1,), (1,)), ((), ())), preferred_element_type=jnp.float32)
    route_grad = jnp.sum(back_hidden * hidden.astype(jnp.float32), axis=1).astype(jnp.bfloat16)
    weight_col = weight.astype(jnp.float32)[:, None]
    scaled = weight_col * back_hidden
    grad_gate = scaled * up_pre * sigmoid_gate * (1.0 + gate_pre * (1.0 - sigmoid_gate))
    grad_up = scaled * active
    grad_pre = jnp.concatenate([grad_gate, grad_up], axis=1).astype(jnp.bfloat16)
    route_input = lax.dot_general(grad_pre, gate_up, (((1,), (1,)), ((), ())), preferred_element_type=jnp.float32).astype(jnp.bfloat16)
    scaled_hidden = (weight_col * hidden.astype(jnp.float32)).astype(jnp.bfloat16)
    return route_input, route_grad, grad_pre, scaled_hidden


def reference(tokens, out_grad, expert_ids, route_weight, w_gate_up, w_down):
    blocks = TOKENS // TOK_DEV
    per_block = TOK_DEV * TOP
    route_experts = expert_ids.reshape(blocks, per_block).astype(jnp.int32)
    onehot = (route_experts[:, :, None] == jnp.arange(EXPERTS, dtype=jnp.int32)[None, None, :]).astype(jnp.int32)
    slot_index = jnp.sum((jnp.cumsum(onehot, axis=1) - onehot) * onehot, axis=2).astype(jnp.int32)
    block_id = jnp.arange(blocks, dtype=jnp.int32)[:, None]
    position = route_experts * (blocks * CAP) + block_id * CAP + slot_index
    route_index = jnp.arange(TOKENS * TOP, dtype=jnp.int32).reshape(blocks, per_block)
    sentinel = TOKENS * TOP
    source_table = jnp.full((EXPERTS * blocks * CAP,), sentinel, jnp.int32)
    source_table = source_table.at[position.reshape(-1)].set(route_index.reshape(-1))
    source_table = source_table.reshape(EXPERTS, blocks * CAP)
    weights_flat = route_weight.reshape(-1)

    def per_expert(state_pair, inputs):
        grad_tokens, grad_route = state_pair
        routes, gate_up, down = inputs
        token_of = (routes // TOP).astype(jnp.int32)
        rows_in = jnp.take(tokens, token_of, axis=0, mode="fill", fill_value=0)
        rows_grad = jnp.take(out_grad, token_of, axis=0, mode="fill", fill_value=0)
        weight = jnp.take(weights_flat, routes, axis=0, mode="fill", fill_value=0)
        route_input, route_grad, grad_pre, scaled_hidden = expert_backward(rows_in, rows_grad, weight, gate_up, down)
        grad_tokens = grad_tokens.at[token_of].add(route_input.astype(jnp.float32), mode="drop")
        grad_route = grad_route.at[routes].set(route_grad, mode="drop")
        shaped_in = rows_in.reshape(N_EXPERT, N_DP, CAP, D).astype(jnp.float32)
        shaped_pre = grad_pre.reshape(N_EXPERT, N_DP, CAP, 2 * FF).astype(jnp.float32)
        shaped_hidden = scaled_hidden.reshape(N_EXPERT, N_DP, CAP, FF).astype(jnp.float32)
        shaped_grad = rows_grad.reshape(N_EXPERT, N_DP, CAP, D).astype(jnp.float32)
        partial_gate_up = jnp.einsum("edcx,edcf->dxf", shaped_in, shaped_pre).astype(jnp.bfloat16)
        partial_down = jnp.einsum("edcf,edcx->dfx", shaped_hidden, shaped_grad).astype(jnp.bfloat16)
        mean_gate_up = (jnp.sum(partial_gate_up.astype(jnp.float32), axis=0) / N_DP).astype(jnp.bfloat16)
        mean_down = (jnp.sum(partial_down.astype(jnp.float32), axis=0) / N_DP).astype(jnp.bfloat16)
        return (grad_tokens, grad_route), (mean_gate_up, mean_down)

    start = (jnp.zeros((TOKENS, D), jnp.float32), jnp.zeros((TOKENS * TOP,), jnp.bfloat16))
    final, stacked = lax.scan(per_expert, start, (source_table, w_gate_up, w_down))
    grad_tokens, grad_route = final
    grad_gate_up, grad_down = stacked
    return grad_tokens.astype(jnp.bfloat16), grad_route.reshape(TOKENS, TOP), grad_gate_up, grad_down
```

```python
import functools
import jax
import jax.numpy as jnp
from jax import lax
from jax.experimental import pallas as pl
from jax.experimental.pallas import tpu as pltpu
from jax.sharding import PartitionSpec as P

MESH = pl.DeviceIdType.MESH
PAD = 128


def fused_kernel(tok, gaug, wgu, wd, t_all, g_all, o_gu, o_dn, o_tok,
                 xbuf, gbuf, gp, sh, dr, acc_gu, acc_dn, part, half, last,
                 rt, rg, st, sg, zt, zg, loc, pr, ps, fr, fs):
    rows = tok.shape[0]
    dm = tok.shape[1]
    e = lax.axis_index("expert")
    z = lax.axis_index("dp")
    e_c = e + 1 - 2 * (e % 2)
    e_x = e + 2 - 4 * ((e // 2) % 2)
    e_y = e + 4 - 8 * ((e // 4) % 2)
    e_xy = e_y + 2 - 4 * ((e // 2) % 2)
    z_off = (z, z + 1 - 2 * (z % 2), z + 2 - 4 * (z // 2), 3 - z)

    barrier = pltpu.get_barrier_semaphore()
    for peer in ((e_c, z), (e_x, z), (e_y, z), (e_xy, z), (e, z_off[1]), (e, z_off[2]), (e, z_off[3])):
        pl.semaphore_signal(barrier, inc=1, device_id=peer, device_id_type=MESH)
    pl.semaphore_wait(barrier, 7)

    def blk(buf, u, k):
        return buf.at[u, pl.ds(k * rows, rows)]

    def copy(buf, recv, send, kind, su, sk, du, dk, dev):
        return pltpu.make_async_remote_copy(
            src_ref=blk(buf, su, sk), dst_ref=blk(buf, du, dk),
            send_sem=send.at[kind, su, sk], recv_sem=recv.at[du, dk],
            device_id=(dev, z), device_id_type=MESH)

    def t_x(u, k): return copy(t_all, rt, st, 0, u, k, u, k + 1, e_x)
    def t_y(u, k): return copy(t_all, rt, st, 1, u, k, u, k + 2, e_y)
    def t_c(u, k): return copy(t_all, rt, st, 2, u, k, u + 1, k, e_c)
    def g_x(u, k): return copy(g_all, rg, sg, 0, u, k, u, k + 1, e_x)
    def g_y(u, k): return copy(g_all, rg, sg, 1, u, k, u, k + 2, e_y)
    def g_c(u, k): return copy(g_all, rg, sg, 2, u, k, u + 1, k, e_c)

    def zcopy(buf, recv, send, dz):
        return pltpu.make_async_remote_copy(
            src_ref=blk(buf, 0, 0), dst_ref=blk(buf, 2 * dz, 0),
            send_sem=send.at[dz - 1], recv_sem=recv.at[2 * dz, 0],
            device_id=(e, z_off[dz]), device_id_type=MESH)

    def got(buf, recv, u, k):
        pltpu.make_async_remote_copy(
            src_ref=blk(buf, u, k), dst_ref=blk(buf, u, k),
            send_sem=zt.at[0], recv_sem=recv.at[u, k],
            device_id=(e_c, z), device_id_type=MESH).wait_recv()

    def issue(u):
        t_x(u, 0).start()
        g_y(u, 0).start()
        t_y(u, 0).start()
        g_x(u, 0).start()
        t_c(u, 0).start()
        g_c(u, 0).start()

    a = pltpu.make_async_copy(tok, blk(t_all, 0, 0), loc.at[0])
    b = pltpu.make_async_copy(gaug, blk(g_all, 0, 0), loc.at[1])
    a.start()
    b.start()
    a.wait()
    b.wait()
    issue(0)
    for dz in (1, 2, 3):
        zcopy(t_all, rt, zt, dz).start()
        zcopy(g_all, rg, zg, dz).start()
    acc_gu[...] = jnp.zeros_like(acc_gu)
    acc_dn[...] = jnp.zeros_like(acc_dn)

    width_gu = acc_gu.shape[1]
    width_dn = acc_dn.shape[2]
    ff = wd.shape[1]
    count = wgu.shape[0]

    def unit(u):
        ca = pltpu.make_async_copy(t_all.at[u], xbuf, loc.at[0])
        cb = pltpu.make_async_copy(g_all.at[u], gbuf, loc.at[1])
        ca.start()
        cb.start()
        ca.wait()
        cb.wait()
        dr[...] = jnp.zeros_like(dr)

        @pl.loop(0, count)
        def _(j):
            lane = lax.broadcasted_iota(jnp.int32, (xbuf.shape[0], PAD), 1)
            mine = lane == e * count + j
            tail = gbuf[:, dm:].astype(jnp.float32)
            wcol = jnp.sum(jnp.where(mine, tail, 0.0), axis=1, keepdims=True)
            pre = jnp.dot(xbuf[...], wgu[j], preferred_element_type=jnp.float32)
            back = lax.dot_general(gbuf[:, :dm], wd[j], (((1,), (1,)), ((), ())),
                                   preferred_element_type=jnp.float32)
            gate = pre[:, :ff]
            up = pre[:, ff:]
            sig = jax.nn.sigmoid(gate)
            act = gate * sig
            hid = (act * up).astype(jnp.bfloat16).astype(jnp.float32)
            dr[...] += jnp.where(mine, jnp.sum(back * hid, axis=1, keepdims=True), 0.0)
            sc = wcol * back
            gp[j, :, :ff] = (sc * up * sig * (1.0 + gate * (1.0 - sig))).astype(jnp.bfloat16)
            gp[j, :, ff:] = (sc * act).astype(jnp.bfloat16)
            sh[...] = (wcol * hid).astype(jnp.bfloat16)
            cols = pl.ds(pl.multiple_of(z * width_gu, 128), width_gu)
            cold = pl.ds(pl.multiple_of(z * width_dn, 128), width_dn)
            acc_gu[j] += lax.dot_general(xbuf[:, cols], gp[j], (((0,), (0,)), ((), ())),
                                         preferred_element_type=jnp.float32)
            acc_dn[j] += lax.dot_general(sh[...], gbuf[:, cold], (((0,), (0,)), ((), ())),
                                         preferred_element_type=jnp.float32)

    def partial(c):
        step = 512

        @pl.loop(0, dm // step)
        def _(n):
            cols = pl.ds(pl.multiple_of(n * step, 128), step)
            total = lax.dot_general(gp[0], wgu[0, cols, :], (((1,), (1,)), ((), ())),
                                    preferred_element_type=jnp.float32)
            for j in range(1, count):
                total += lax.dot_general(gp[j], wgu[j, cols, :], (((1,), (1,)), ((), ())),
                                         preferred_element_type=jnp.float32)
            part[c, :, cols] = total.astype(jnp.bfloat16)
        part[c, :, dm:] = dr[...].astype(jnp.bfloat16)

    to_core = pltpu.make_async_remote_copy(
        src_ref=part.at[1], dst_ref=half, send_sem=ps, recv_sem=pr,
        device_id=(e_c, z), device_id_type=MESH)
    to_owner = [pltpu.make_async_remote_copy(
        src_ref=part.at[0, pl.ds(k * rows, rows)], dst_ref=last.at[k - 1],
        send_sem=fs.at[k - 1], recv_sem=fr.at[k - 1],
        device_id=(dev, z), device_id_type=MESH) for k, dev in ((1, e_x), (2, e_y), (3, e_xy))]

    @pl.loop(0, 5)
    def _(i):
        u = 2 * i

        @pl.when(i > 0)
        def _():
            unit(2 * i - 1)

        @pl.when(i == 1)
        def _():
            partial(1)
            to_core.start()

        @pl.when(i < 4)
        def _():
            got(t_all, rt, u, 1)
            t_y(u, 1).start()
            t_c(u, 1).start()
            got(g_all, rg, u, 2)
            g_x(u, 2).start()
            g_c(u, 2).start()

        @pl.when(i > 0)
        def _():
            unit(2 * i - 2)

        @pl.when(i == 1)
        def _():
            partial(0)
            to_core.wait_recv()
            part[0] = (part[0].astype(jnp.float32) + half[...].astype(jnp.float32)).astype(jnp.bfloat16)
            for c in to_owner:
                c.start()

        @pl.when(i < 4)
        def _():
            got(g_all, rg, u, 1)
            g_c(u, 1).start()
            got(t_all, rt, u, 2)
            t_c(u, 2).start()

        @pl.when(i < 3)
        def _():
            got(t_all, rt, u + 2, 0)
            got(g_all, rg, u + 2, 0)
            issue(u + 2)

        @pl.when(i < 4)
        def _():
            got(t_all, rt, u, 3)
            t_c(u, 3).start()
            got(g_all, rg, u, 3)
            g_c(u, 3).start()
            for k in range(4):
                got(t_all, rt, u + 1, k)
                got(g_all, rg, u + 1, k)

    o_gu[...] = (acc_gu[...] * (1.0 / lax.axis_size("dp"))).astype(jnp.bfloat16)
    o_dn[...] = (acc_dn[...] * (1.0 / lax.axis_size("dp"))).astype(jnp.bfloat16)
    for c in to_owner:
        c.wait_recv()
    total = part[0, pl.ds(0, rows), :].astype(jnp.float32)
    for k in range(3):
        total += last[k].astype(jnp.float32)
    o_tok[...] = total.astype(jnp.bfloat16)

    to_core.wait_send()
    for c in to_owner:
        c.wait_send()
    for dz in (1, 2, 3):
        zcopy(t_all, rt, zt, dz).wait_send()
        zcopy(g_all, rg, zg, dz).wait_send()

    @pl.loop(0, 4)
    def _(i):
        u = 2 * i
        for c in (t_x(u, 0), t_y(u, 0), t_y(u, 1), g_x(u, 0), g_y(u, 0), g_x(u, 2)):
            c.wait_send()
        for k in range(4):
            t_c(u, k).wait_send()
            g_c(u, k).wait_send()


def local_fused(tokens, out_grad, expert_ids, route_weight, w_gate_up, w_down):
    rows, dm = tokens.shape
    count, _, width = w_gate_up.shape
    ff = w_down.shape[1]
    n_dp = lax.axis_size("dp")
    units = 2 * n_dp
    lanes = jnp.arange(PAD, dtype=jnp.int32)
    onehot = expert_ids[:, :, None] == lanes[None, None, :]
    dense = jnp.sum(jnp.where(onehot, route_weight[:, :, None].astype(jnp.float32), 0.0), axis=1)
    gaug = jnp.concatenate([out_grad, dense.astype(jnp.bfloat16)], axis=1)
    bf, f32 = jnp.bfloat16, jnp.float32
    dma = pltpu.SemaphoreType.DMA
    vm = pl.BlockSpec(memory_space=pltpu.VMEM)
    anyw = pl.BlockSpec(memory_space=pl.ANY)
    _, _, o_gu, o_dn, o_tok = pl.pallas_call(
        fused_kernel,
        out_shape=(
            jax.ShapeDtypeStruct((units, 4 * rows, dm), bf),
            jax.ShapeDtypeStruct((units, 4 * rows, dm + PAD), bf),
            jax.ShapeDtypeStruct((count, dm // n_dp, width), bf),
            jax.ShapeDtypeStruct((count, ff, dm // n_dp), bf),
            jax.ShapeDtypeStruct((rows, dm + PAD), bf),
        ),
        in_specs=[vm] * 4,
        out_specs=(anyw, anyw, vm, vm, vm),
        scratch_shapes=[
            pltpu.VMEM((4 * rows, dm), bf),
            pltpu.VMEM((4 * rows, dm + PAD), bf),
            pltpu.VMEM((count, 4 * rows, width), bf),
            pltpu.VMEM((4 * rows, ff), bf),
            pltpu.VMEM((4 * rows, PAD), f32),
            pltpu.VMEM((count, dm // n_dp, width), f32),
            pltpu.VMEM((count, ff, dm // n_dp), f32),
            pltpu.VMEM((2, 4 * rows, dm + PAD), bf),
            pltpu.VMEM((4 * rows, dm + PAD), bf),
            pltpu.VMEM((3, rows, dm + PAD), bf),
            dma((units, 4)), dma((units, 4)), dma((3, units, 4)), dma((3, units, 4)),
            dma((3,)), dma((3,)), dma((2,)),
            dma, dma, dma((3,)), dma((3,)),
        ],
        compiler_params=pltpu.CompilerParams(
            collective_id=0, has_side_effects=True, vmem_limit_bytes=60 * 1024 * 1024),
    )(tokens, gaug, w_gate_up, w_down)
    d_route = jnp.sum(jnp.where(onehot, o_tok[:, None, dm:].astype(f32), 0.0), axis=2).astype(bf)
    return o_tok[:, :dm], d_route, o_gu, o_dn


def expert_backward(rows_in, rows_grad, weight, gate_up, down):
    pre_act = jnp.dot(rows_in, gate_up, preferred_element_type=jnp.float32)
    half_width = pre_act.shape[1] // 2
    gate_pre = pre_act[:, :half_width]
    up_pre = pre_act[:, half_width:]
    sigmoid_gate = jax.nn.sigmoid(gate_pre)
    active = gate_pre * sigmoid_gate
    hidden = (active * up_pre).astype(jnp.bfloat16)
    back_hidden = lax.dot_general(
        rows_grad, down, (((1,), (1,)), ((), ())), preferred_element_type=jnp.float32
    )
    route_grad = jnp.sum(back_hidden * hidden.astype(jnp.float32), axis=1).astype(jnp.bfloat16)
    weight_col = weight.astype(jnp.float32)[:, None]
    scaled = weight_col * back_hidden
    grad_gate = scaled * up_pre * sigmoid_gate * (1.0 + gate_pre * (1.0 - sigmoid_gate))
    grad_up = scaled * active
    grad_pre = jnp.concatenate([grad_gate, grad_up], axis=1).astype(jnp.bfloat16)
    route_input = lax.dot_general(
        grad_pre, gate_up, (((1,), (1,)), ((), ())), preferred_element_type=jnp.float32
    ).astype(jnp.bfloat16)
    scaled_hidden = (weight_col * hidden.astype(jnp.float32)).astype(jnp.bfloat16)
    return (route_input, route_grad, grad_pre, scaled_hidden)


def weight_terms(rows_in, rows_grad, grad_pre, scaled_hidden):
    term_gate_up = lax.dot_general(
        rows_in, grad_pre, (((0,), (0,)), ((), ())), preferred_element_type=jnp.float32
    )
    term_down = lax.dot_general(
        scaled_hidden, rows_grad, (((0,), (0,)), ((), ())), preferred_element_type=jnp.float32
    )
    return (term_gate_up, term_down)


def run_expert(arrived_in, arrived_grad, arrived_weight, gate_up, down):
    groups = arrived_in.shape[0]
    capacity = arrived_in.shape[1]
    dim_model = arrived_in.shape[2]
    rows_in = arrived_in.reshape(groups * capacity, dim_model)
    rows_grad = arrived_grad.reshape(groups * capacity, dim_model)
    weight = arrived_weight.reshape(groups * capacity)
    route_input, route_grad, grad_pre, scaled_hidden = expert_backward(
        rows_in, rows_grad, weight, gate_up, down
    )
    shaped_input = route_input.reshape(groups, capacity, dim_model)
    shaped_grad = route_grad.reshape(groups, capacity)
    return (shaped_input, shaped_grad, (rows_in, rows_grad, grad_pre, scaled_hidden))


def slot_numbers(route_experts, all_experts):
    route_count = route_experts.shape[0]
    block_len = 128
    block_count = route_count // block_len
    onehot = (route_experts[:, None] == jnp.arange(all_experts, dtype=jnp.int32)[None, :]).astype(
        jnp.bfloat16
    )
    onehot = onehot.reshape(block_count, block_len, all_experts)
    lower = (jnp.arange(block_len)[:, None] > jnp.arange(block_len)[None, :]).astype(jnp.bfloat16)
    within = jnp.einsum("ij,bje->bie", lower, onehot, preferred_element_type=jnp.float32)
    totals = jnp.sum(onehot.astype(jnp.float32), axis=1)
    earlier = (jnp.arange(block_count)[:, None] > jnp.arange(block_count)[None, :]).astype(
        jnp.float32
    )
    before = jnp.dot(earlier, totals, precision=lax.Precision.HIGHEST)
    counted = jnp.sum((within + before[:, None, :]) * onehot.astype(jnp.float32), axis=2)
    return counted.reshape(route_count).astype(jnp.int32)


def local(tokens, out_grad, expert_ids, route_weight, w_gate_up, w_down):
    tok_rows = tokens.shape[0]
    dim_model = tokens.shape[1]
    top_count = expert_ids.shape[1]
    exp_local = w_gate_up.shape[0]
    groups = lax.axis_size("expert")
    all_experts = exp_local * groups
    route_count = tok_rows * top_count
    capacity = 9 * tok_rows * top_count // (8 * all_experts)
    route_experts = expert_ids.reshape(route_count)
    slot_index = slot_numbers(route_experts, all_experts)
    target = route_experts // exp_local
    local_expert = route_experts % exp_local
    position = local_expert * (groups * capacity) + target * capacity + slot_index
    source_table = jnp.full((all_experts * capacity,), route_count, jnp.int32)
    source_table = source_table.at[position].set(jnp.arange(route_count, dtype=jnp.int32))
    token_of = source_table // top_count
    send_in = jnp.take(tokens, token_of, axis=0, mode="fill", fill_value=0).reshape(
        exp_local, groups, capacity, dim_model
    )
    send_grad = jnp.take(out_grad, token_of, axis=0, mode="fill", fill_value=0).reshape(
        exp_local, groups, capacity, dim_model
    )
    send_weight = jnp.take(
        route_weight.reshape(route_count), source_table, axis=0, mode="fill", fill_value=0
    ).reshape(exp_local, groups, capacity)
    gate_up_terms = []
    down_terms = []
    arrived_in, arrived_grad, arrived_weight = (
        lax.all_to_all(send_in, "expert", split_axis=1, concat_axis=1, tiled=True),
        lax.all_to_all(send_grad, "expert", split_axis=1, concat_axis=1, tiled=True),
        lax.all_to_all(send_weight, "expert", split_axis=1, concat_axis=1, tiled=True),
    )
    inputs_list = []
    grads_list = []
    saved = []
    for which in range(exp_local):
        shaped_input, shaped_grad, kept = run_expert(
            arrived_in[which],
            arrived_grad[which],
            arrived_weight[which],
            w_gate_up[which],
            w_down[which],
        )
        inputs_list.append(shaped_input)
        grads_list.append(shaped_grad)
        saved.append(kept)
    returned_in, returned_route = (
        lax.all_to_all(jnp.stack(inputs_list), "expert", split_axis=1, concat_axis=1, tiled=True),
        lax.all_to_all(jnp.stack(grads_list), "expert", split_axis=1, concat_axis=1, tiled=True),
    )
    for which in range(exp_local):
        term_gate_up, term_down = weight_terms(*saved[which])
        gate_up_terms.append(term_gate_up)
        down_terms.append(term_down)
    summed_gate_up, summed_down = (
        lax.psum_scatter(
            jnp.stack(gate_up_terms).astype(jnp.bfloat16), "dp", scatter_dimension=1, tiled=True
        ).astype(jnp.float32),
        lax.psum_scatter(
            jnp.stack(down_terms).astype(jnp.bfloat16), "dp", scatter_dimension=2, tiled=True
        ).astype(jnp.float32),
    )
    mean_factor = 1.0 / lax.axis_size("dp")
    grad_gate_up = (summed_gate_up * mean_factor).astype(jnp.bfloat16)
    grad_down = (summed_down * mean_factor).astype(jnp.bfloat16)
    back_flat = returned_in.reshape(all_experts * capacity, dim_model)
    route_flat = returned_route.reshape(all_experts * capacity)
    route_rows = jnp.take(back_flat, position, axis=0).reshape(tok_rows, top_count, dim_model)
    d_tokens = jnp.sum(route_rows.astype(jnp.float32), axis=1).astype(jnp.bfloat16)
    d_route = jnp.take(route_flat, position, axis=0).reshape(tok_rows, top_count)
    return (d_tokens, d_route, grad_gate_up, grad_down)


def solution(mesh):
    placed = (
        P(("expert", "dp"), None),
        P(("expert", "dp"), None),
        P(("expert", "dp"), None),
        P(("expert", "dp"), None),
        P("expert", None, None),
        P("expert", None, None),
    )
    small = mesh.shape["expert"] == 8 and mesh.shape["dp"] == 4
    return jax.shard_map(
        local_fused if small else local,
        mesh=mesh,
        in_specs=placed,
        out_specs=(
            P(("expert", "dp"), None),
            P(("expert", "dp"), None),
            P("expert", "dp", None),
            P("expert", None, "dp"),
        ),
        check_vma=False,
    )
```

```python
import functools
import jax
import jax.numpy as jnp
from jax import lax
from jax.experimental import pallas as pl
from jax.experimental.pallas import tpu as pltpu
from jax.sharding import PartitionSpec as P

MESH = pl.DeviceIdType.MESH
PAD = 128


def fused_kernel(tok, gaug, wgu, wd, t_all, g_all, o_gu, o_dn, o_tok, o_dr,
                 xbuf, gbuf, gp, sh, dr, acc_gu, acc_dn, part, half, last,
                 rt, rg, st, sg, zt, zg, loc, pr, ps, fr, fs):
    rows = tok.shape[0]
    dm = tok.shape[1]
    e = lax.axis_index("expert")
    z = lax.axis_index("dp")
    e_c = e + 1 - 2 * (e % 2)
    e_x = e + 2 - 4 * ((e // 2) % 2)
    e_y = e + 4 - 8 * ((e // 4) % 2)
    e_xy = e_y + 2 - 4 * ((e // 2) % 2)
    z_off = (z, z + 1 - 2 * (z % 2), z + 2 - 4 * (z // 2), 3 - z)

    barrier = pltpu.get_barrier_semaphore()
    for peer in ((e_c, z), (e_x, z), (e_y, z), (e_xy, z), (e, z_off[1]), (e, z_off[2]), (e, z_off[3])):
        pl.semaphore_signal(barrier, inc=1, device_id=peer, device_id_type=MESH)
    pl.semaphore_wait(barrier, 7)

    def blk(buf, u, k):
        return buf.at[u, pl.ds(k * rows, rows)]

    def copy(buf, recv, send, kind, su, sk, du, dk, dev):
        return pltpu.make_async_remote_copy(
            src_ref=blk(buf, su, sk), dst_ref=blk(buf, du, dk),
            send_sem=send.at[kind, su, sk], recv_sem=recv.at[du, dk],
            device_id=(dev, z), device_id_type=MESH)

    def t_x(u, k): return copy(t_all, rt, st, 0, u, k, u, k + 1, e_x)
    def t_y(u, k): return copy(t_all, rt, st, 1, u, k, u, k + 2, e_y)
    def t_c(u, k): return copy(t_all, rt, st, 2, u, k, u + 1, k, e_c)
    def g_x(u, k): return copy(g_all, rg, sg, 0, u, k, u, k + 1, e_x)
    def g_y(u, k): return copy(g_all, rg, sg, 1, u, k, u, k + 2, e_y)
    def g_c(u, k): return copy(g_all, rg, sg, 2, u, k, u + 1, k, e_c)

    def zcopy(buf, recv, send, dz):
        return pltpu.make_async_remote_copy(
            src_ref=blk(buf, 0, 0), dst_ref=blk(buf, 2 * dz, 0),
            send_sem=send.at[dz - 1], recv_sem=recv.at[2 * dz, 0],
            device_id=(e, z_off[dz]), device_id_type=MESH)

    def got(buf, recv, u, k):
        pltpu.make_async_remote_copy(
            src_ref=blk(buf, u, k), dst_ref=blk(buf, u, k),
            send_sem=zt.at[0], recv_sem=recv.at[u, k],
            device_id=(e_c, z), device_id_type=MESH).wait_recv()

    def issue(u):
        t_x(u, 0).start()
        g_y(u, 0).start()
        t_y(u, 0).start()
        g_x(u, 0).start()
        t_c(u, 0).start()
        g_c(u, 0).start()

    a = pltpu.make_async_copy(tok, blk(t_all, 0, 0), loc.at[0])
    b = pltpu.make_async_copy(gaug, blk(g_all, 0, 0), loc.at[1])
    a.start()
    b.start()
    a.wait()
    b.wait()
    issue(0)
    for dz in (1, 2, 3):
        zcopy(t_all, rt, zt, dz).start()
        zcopy(g_all, rg, zg, dz).start()
    acc_gu[...] = jnp.zeros_like(acc_gu)
    acc_dn[...] = jnp.zeros_like(acc_dn)

    width_gu = acc_gu.shape[1]
    width_dn = acc_dn.shape[2]
    ff = wd.shape[1]
    count = wgu.shape[0]

    def unit(u, c, h):
        own = pl.ds(h * 2 * rows, 2 * rows)
        ca = pltpu.make_async_copy(t_all.at[u, own], xbuf, loc.at[0])
        cb = pltpu.make_async_copy(g_all.at[u, own], gbuf, loc.at[1])
        ca.start()
        cb.start()
        ca.wait()
        cb.wait()
        dr[c, own] = jnp.zeros((2 * rows, PAD), jnp.float32)

        @pl.loop(0, count)
        def _(j):
            lane = lax.broadcasted_iota(jnp.int32, (xbuf.shape[0], PAD), 1)
            mine = lane == e * count + j
            tail = gbuf[:, dm:].astype(jnp.float32)
            wcol = jnp.sum(jnp.where(mine, tail, 0.0), axis=1, keepdims=True)
            pre = jnp.dot(xbuf[...], wgu[j], preferred_element_type=jnp.float32)
            back = lax.dot_general(gbuf[:, :dm], wd[j], (((1,), (1,)), ((), ())),
                                   preferred_element_type=jnp.float32)
            gate = pre[:, :ff]
            up = pre[:, ff:]
            sig = jax.nn.sigmoid(gate)
            act = gate * sig
            hid = (act * up).astype(jnp.bfloat16).astype(jnp.float32)
            dr[c, own] += jnp.where(mine, jnp.sum(back * hid, axis=1, keepdims=True), 0.0)
            sc = wcol * back
            gp[c, j, own, :ff] = (sc * up * sig * (1.0 + gate * (1.0 - sig))).astype(jnp.bfloat16)
            gp[c, j, own, ff:] = (sc * act).astype(jnp.bfloat16)
            sh[...] = (wcol * hid).astype(jnp.bfloat16)
            cols = pl.ds(pl.multiple_of(z * width_gu, 128), width_gu)
            cold = pl.ds(pl.multiple_of(z * width_dn, 128), width_dn)
            acc_gu[j] += lax.dot_general(xbuf[:, cols], gp[c, j, own], (((0,), (0,)), ((), ())),
                                         preferred_element_type=jnp.float32)
            acc_dn[j] += lax.dot_general(sh[...], gbuf[:, cold], (((0,), (0,)), ((), ())),
                                         preferred_element_type=jnp.float32)

    def partial(c):
        step = 512

        @pl.loop(0, dm // step)
        def _(n):
            cols = pl.ds(pl.multiple_of(n * step, 128), step)
            total = lax.dot_general(gp[c, 0], wgu[0, cols, :], (((1,), (1,)), ((), ())),
                                    preferred_element_type=jnp.float32)
            for j in range(1, count):
                total += lax.dot_general(gp[c, j], wgu[j, cols, :], (((1,), (1,)), ((), ())),
                                         preferred_element_type=jnp.float32)
            part[c, :, cols] = total.astype(jnp.bfloat16)
        part[c, :, dm:] = dr[c].astype(jnp.bfloat16)

    to_core = pltpu.make_async_remote_copy(
        src_ref=part.at[1], dst_ref=half, send_sem=ps, recv_sem=pr,
        device_id=(e_c, z), device_id_type=MESH)
    to_owner = [pltpu.make_async_remote_copy(
        src_ref=part.at[0, pl.ds(k * rows, rows)], dst_ref=last.at[k - 1],
        send_sem=fs.at[k - 1], recv_sem=fr.at[k - 1],
        device_id=(dev, z), device_id_type=MESH) for k, dev in ((1, e_x), (2, e_y), (3, e_xy))]

    @pl.loop(0, 5)
    def _(i):
        u = 2 * i

        @pl.when(i > 0)
        def _():
            unit(2 * i - 1, 1, 1)

        @pl.when(i == 1)
        def _():
            partial(1)
            to_core.start()

        @pl.when(i < 4)
        def _():
            got(t_all, rt, u, 1)
            t_y(u, 1).start()
            t_c(u, 1).start()
            got(g_all, rg, u, 2)
            g_x(u, 2).start()
            g_c(u, 2).start()

        @pl.when(i > 0)
        def _():
            unit(2 * i - 2, 0, 1)

        @pl.when(i == 1)
        def _():
            partial(0)
            to_core.wait_recv()
            part[0] = (part[0].astype(jnp.float32) + half[...].astype(jnp.float32)).astype(jnp.bfloat16)
            for c in to_owner:
                c.start()

        @pl.when(i < 4)
        def _():
            got(g_all, rg, u, 1)
            g_c(u, 1).start()
            got(t_all, rt, u, 2)
            t_c(u, 2).start()

        @pl.when(i < 3)
        def _():
            got(t_all, rt, u + 2, 0)
            got(g_all, rg, u + 2, 0)
            issue(u + 2)

        @pl.when(i < 4)
        def _():
            unit(u, 0, 0)
            for k in range(2):
                got(t_all, rt, u + 1, k)
                got(g_all, rg, u + 1, k)
            unit(u + 1, 1, 0)
            got(t_all, rt, u, 3)
            t_c(u, 3).start()
            got(g_all, rg, u, 3)
            g_c(u, 3).start()
            for k in (2, 3):
                got(t_all, rt, u + 1, k)
                got(g_all, rg, u + 1, k)

    o_gu[...] = (acc_gu[...] * (1.0 / lax.axis_size("dp"))).astype(jnp.bfloat16)
    o_dn[...] = (acc_dn[...] * (1.0 / lax.axis_size("dp"))).astype(jnp.bfloat16)
    for c in to_owner:
        c.wait_recv()
    total = part[0, pl.ds(0, rows), :].astype(jnp.float32)
    for k in range(3):
        total += last[k].astype(jnp.float32)
    o_tok[...] = total[:, :dm].astype(jnp.bfloat16)
    o_dr[...] = total[:, dm:].astype(jnp.bfloat16)

    to_core.wait_send()
    for c in to_owner:
        c.wait_send()
    for dz in (1, 2, 3):
        zcopy(t_all, rt, zt, dz).wait_send()
        zcopy(g_all, rg, zg, dz).wait_send()

    @pl.loop(0, 4)
    def _(i):
        u = 2 * i
        for c in (t_x(u, 0), t_y(u, 0), t_y(u, 1), g_x(u, 0), g_y(u, 0), g_x(u, 2)):
            c.wait_send()
        for k in range(4):
            t_c(u, k).wait_send()
            g_c(u, k).wait_send()


def local_fused(tokens, out_grad, expert_ids, route_weight, w_gate_up, w_down):
    rows, dm = tokens.shape
    count, _, width = w_gate_up.shape
    ff = w_down.shape[1]
    n_dp = lax.axis_size("dp")
    units = 2 * n_dp
    lanes = jnp.arange(PAD, dtype=jnp.int32)
    onehot = expert_ids[:, :, None] == lanes[None, None, :]
    dense = jnp.sum(jnp.where(onehot, route_weight[:, :, None].astype(jnp.float32), 0.0), axis=1)
    gaug = jnp.concatenate([out_grad, dense.astype(jnp.bfloat16)], axis=1)
    bf, f32 = jnp.bfloat16, jnp.float32
    dma = pltpu.SemaphoreType.DMA
    vm = pl.BlockSpec(memory_space=pltpu.VMEM)
    anyw = pl.BlockSpec(memory_space=pl.ANY)
    _, _, o_gu, o_dn, o_tok, o_dr = pl.pallas_call(
        fused_kernel,
        out_shape=(
            jax.ShapeDtypeStruct((units, 4 * rows, dm), bf),
            jax.ShapeDtypeStruct((units, 4 * rows, dm + PAD), bf),
            jax.ShapeDtypeStruct((count, dm // n_dp, width), bf),
            jax.ShapeDtypeStruct((count, ff, dm // n_dp), bf),
            jax.ShapeDtypeStruct((rows, dm), bf),
            jax.ShapeDtypeStruct((rows, PAD), bf),
        ),
        in_specs=[vm] * 4,
        out_specs=(anyw, anyw, vm, vm, vm, vm),
        scratch_shapes=[
            pltpu.VMEM((2 * rows, dm), bf),
            pltpu.VMEM((2 * rows, dm + PAD), bf),
            pltpu.VMEM((2, count, 4 * rows, width), bf),
            pltpu.VMEM((2 * rows, ff), bf),
            pltpu.VMEM((2, 4 * rows, PAD), f32),
            pltpu.VMEM((count, dm // n_dp, width), f32),
            pltpu.VMEM((count, ff, dm // n_dp), f32),
            pltpu.VMEM((2, 4 * rows, dm + PAD), bf),
            pltpu.VMEM((4 * rows, dm + PAD), bf),
            pltpu.VMEM((3, rows, dm + PAD), bf),
            dma((units, 4)), dma((units, 4)), dma((3, units, 4)), dma((3, units, 4)),
            dma((3,)), dma((3,)), dma((2,)),
            dma, dma, dma((3,)), dma((3,)),
        ],
        compiler_params=pltpu.CompilerParams(
            collective_id=0, has_side_effects=True, vmem_limit_bytes=60 * 1024 * 1024),
    )(tokens, gaug, w_gate_up, w_down)
    d_route = jnp.sum(jnp.where(onehot, o_dr[:, None, :].astype(f32), 0.0), axis=2).astype(bf)
    return o_tok, d_route, o_gu, o_dn


def expert_backward(rows_in, rows_grad, weight, gate_up, down):
    pre_act = jnp.dot(rows_in, gate_up, preferred_element_type=jnp.float32)
    half_width = pre_act.shape[1] // 2
    gate_pre = pre_act[:, :half_width]
    up_pre = pre_act[:, half_width:]
    sigmoid_gate = jax.nn.sigmoid(gate_pre)
    active = gate_pre * sigmoid_gate
    hidden = (active * up_pre).astype(jnp.bfloat16)
    back_hidden = lax.dot_general(
        rows_grad, down, (((1,), (1,)), ((), ())), preferred_element_type=jnp.float32
    )
    route_grad = jnp.sum(back_hidden * hidden.astype(jnp.float32), axis=1).astype(jnp.bfloat16)
    weight_col = weight.astype(jnp.float32)[:, None]
    scaled = weight_col * back_hidden
    grad_gate = scaled * up_pre * sigmoid_gate * (1.0 + gate_pre * (1.0 - sigmoid_gate))
    grad_up = scaled * active
    grad_pre = jnp.concatenate([grad_gate, grad_up], axis=1).astype(jnp.bfloat16)
    route_input = lax.dot_general(
        grad_pre, gate_up, (((1,), (1,)), ((), ())), preferred_element_type=jnp.float32
    ).astype(jnp.bfloat16)
    scaled_hidden = (weight_col * hidden.astype(jnp.float32)).astype(jnp.bfloat16)
    return (route_input, route_grad, grad_pre, scaled_hidden)


def weight_terms(rows_in, rows_grad, grad_pre, scaled_hidden):
    term_gate_up = lax.dot_general(
        rows_in, grad_pre, (((0,), (0,)), ((), ())), preferred_element_type=jnp.float32
    )
    term_down = lax.dot_general(
        scaled_hidden, rows_grad, (((0,), (0,)), ((), ())), preferred_element_type=jnp.float32
    )
    return (term_gate_up, term_down)


def run_expert(arrived_in, arrived_grad, arrived_weight, gate_up, down):
    groups = arrived_in.shape[0]
    capacity = arrived_in.shape[1]
    dim_model = arrived_in.shape[2]
    rows_in = arrived_in.reshape(groups * capacity, dim_model)
    rows_grad = arrived_grad.reshape(groups * capacity, dim_model)
    weight = arrived_weight.reshape(groups * capacity)
    route_input, route_grad, grad_pre, scaled_hidden = expert_backward(
        rows_in, rows_grad, weight, gate_up, down
    )
    shaped_input = route_input.reshape(groups, capacity, dim_model)
    shaped_grad = route_grad.reshape(groups, capacity)
    return (shaped_input, shaped_grad, (rows_in, rows_grad, grad_pre, scaled_hidden))


def slot_numbers(route_experts, all_experts):
    route_count = route_experts.shape[0]
    block_len = 128
    block_count = route_count // block_len
    onehot = (route_experts[:, None] == jnp.arange(all_experts, dtype=jnp.int32)[None, :]).astype(
        jnp.bfloat16
    )
    onehot = onehot.reshape(block_count, block_len, all_experts)
    lower = (jnp.arange(block_len)[:, None] > jnp.arange(block_len)[None, :]).astype(jnp.bfloat16)
    within = jnp.einsum("ij,bje->bie", lower, onehot, preferred_element_type=jnp.float32)
    totals = jnp.sum(onehot.astype(jnp.float32), axis=1)
    earlier = (jnp.arange(block_count)[:, None] > jnp.arange(block_count)[None, :]).astype(
        jnp.float32
    )
    before = jnp.dot(earlier, totals, precision=lax.Precision.HIGHEST)
    counted = jnp.sum((within + before[:, None, :]) * onehot.astype(jnp.float32), axis=2)
    return counted.reshape(route_count).astype(jnp.int32)


def local(tokens, out_grad, expert_ids, route_weight, w_gate_up, w_down):
    tok_rows = tokens.shape[0]
    dim_model = tokens.shape[1]
    top_count = expert_ids.shape[1]
    exp_local = w_gate_up.shape[0]
    groups = lax.axis_size("expert")
    all_experts = exp_local * groups
    route_count = tok_rows * top_count
    capacity = 9 * tok_rows * top_count // (8 * all_experts)
    route_experts = expert_ids.reshape(route_count)
    slot_index = slot_numbers(route_experts, all_experts)
    target = route_experts // exp_local
    local_expert = route_experts % exp_local
    position = local_expert * (groups * capacity) + target * capacity + slot_index
    source_table = jnp.full((all_experts * capacity,), route_count, jnp.int32)
    source_table = source_table.at[position].set(jnp.arange(route_count, dtype=jnp.int32))
    token_of = source_table // top_count
    send_in = jnp.take(tokens, token_of, axis=0, mode="fill", fill_value=0).reshape(
        exp_local, groups, capacity, dim_model
    )
    send_grad = jnp.take(out_grad, token_of, axis=0, mode="fill", fill_value=0).reshape(
        exp_local, groups, capacity, dim_model
    )
    send_weight = jnp.take(
        route_weight.reshape(route_count), source_table, axis=0, mode="fill", fill_value=0
    ).reshape(exp_local, groups, capacity)
    gate_up_terms = []
    down_terms = []
    arrived_in, arrived_grad, arrived_weight = (
        lax.all_to_all(send_in, "expert", split_axis=1, concat_axis=1, tiled=True),
        lax.all_to_all(send_grad, "expert", split_axis=1, concat_axis=1, tiled=True),
        lax.all_to_all(send_weight, "expert", split_axis=1, concat_axis=1, tiled=True),
    )
    inputs_list = []
    grads_list = []
    saved = []
    for which in range(exp_local):
        shaped_input, shaped_grad, kept = run_expert(
            arrived_in[which],
            arrived_grad[which],
            arrived_weight[which],
            w_gate_up[which],
            w_down[which],
        )
        inputs_list.append(shaped_input)
        grads_list.append(shaped_grad)
        saved.append(kept)
    returned_in, returned_route = (
        lax.all_to_all(jnp.stack(inputs_list), "expert", split_axis=1, concat_axis=1, tiled=True),
        lax.all_to_all(jnp.stack(grads_list), "expert", split_axis=1, concat_axis=1, tiled=True),
    )
    for which in range(exp_local):
        term_gate_up, term_down = weight_terms(*saved[which])
        gate_up_terms.append(term_gate_up)
        down_terms.append(term_down)
    summed_gate_up, summed_down = (
        lax.psum_scatter(
            jnp.stack(gate_up_terms).astype(jnp.bfloat16), "dp", scatter_dimension=1, tiled=True
        ).astype(jnp.float32),
        lax.psum_scatter(
            jnp.stack(down_terms).astype(jnp.bfloat16), "dp", scatter_dimension=2, tiled=True
        ).astype(jnp.float32),
    )
    mean_factor = 1.0 / lax.axis_size("dp")
    grad_gate_up = (summed_gate_up * mean_factor).astype(jnp.bfloat16)
    grad_down = (summed_down * mean_factor).astype(jnp.bfloat16)
    back_flat = returned_in.reshape(all_experts * capacity, dim_model)
    route_flat = returned_route.reshape(all_experts * capacity)
    route_rows = jnp.take(back_flat, position, axis=0).reshape(tok_rows, top_count, dim_model)
    d_tokens = jnp.sum(route_rows.astype(jnp.float32), axis=1).astype(jnp.bfloat16)
    d_route = jnp.take(route_flat, position, axis=0).reshape(tok_rows, top_count)
    return (d_tokens, d_route, grad_gate_up, grad_down)


def solution(mesh):
    placed = (
        P(("expert", "dp"), None),
        P(("expert", "dp"), None),
        P(("expert", "dp"), None),
        P(("expert", "dp"), None),
        P("expert", None, None),
        P("expert", None, None),
    )
    small = mesh.shape["expert"] == 8 and mesh.shape["dp"] == 4
    return jax.shard_map(
        local_fused if small else local,
        mesh=mesh,
        in_specs=placed,
        out_specs=(
            P(("expert", "dp"), None),
            P(("expert", "dp"), None),
            P("expert", "dp", None),
            P("expert", None, "dp"),
        ),
        check_vma=False,
    )
```
